32 devices in a mesh: row: 4 (over y, x), col: 8 (over z, core).
Axes of the slice: x: 2, y: 2, z: 4, core: 2. Of those that a mesh axis runs over, the one named last changes fastest.
Arguments:
- activations: bfloat16 [256, 16384], P(None, 'row'), may hold values from -3 to 3
- cotangent: bfloat16 [256, 16384], P(None, 'row'), may hold values from -0.59765625 to 0.59765625
- forget: int32 [256], replicated, may hold values 0 or 1
- lengths: int32 [4, 4], P('row'), may hold values from 1 to 32, 64 in all within a row
- query_weight: bfloat16 [16384, 8192], P('row', 'col'), may hold values from -0.046875 to 0.046875
- key_weight: bfloat16 [16384, 512], P('row'), may hold values from -0.046875 to 0.046875
- value_weight: bfloat16 [16384, 512], P('row'), may hold values from -0.046875 to 0.046875
- output_projection_weight: bfloat16 [8192, 16384], P('col', 'row'), may hold values from -0.0625 to 0.0625
- query_down: bfloat16 [16384, 32], P('row'), may hold values from -0.046875 to 0.046875
- query_up: bfloat16 [32, 8192], P(None, 'col'), may hold values from -1 to 1
- output_down: bfloat16 [8192, 32], P('col'), may hold values from -0.0625 to 0.0625
- output_up: bfloat16 [32, 16384], P(None, 'row'), may hold values from -1 to 1
Outputs:
- query_down_gradient: float32 [16384, 32], P('row')
- query_up_gradient: float32 [32, 8192], P(None, 'col')
- output_down_gradient: float32 [8192, 32], P('col')
- output_up_gradient: float32 [32, 16384], P(None, 'row')
The draws below stay inside these ranges and needn't reach their ends.
Inputs may be any that keep to these rules, and one draw needn't show every extreme that they name: In every row of lengths the 4 values sum to 64, and the largest is exactly 32.
All inputs are finite; a program needn't handle non-finite values.
Results may differ from the reference program's by a relative error of at most 0.025.
Values may be sent and summed in bfloat16 or wider, within the bound.
A program may use at most 128 MiB of HBM per device.

```python
import math
import jax
import jax.numpy as jnp
import numpy as np
from jax import lax

D = 16384
HD = 128
HEADS = 64
KVH = 4
RANK = 32
SEGS = 4
TOK_BLK = 64
MOST = 32
TOKENS = 256
N_ROW = 4


def set_ends(values, stream_key, smallest, high):
    spot = [jax.random.randint(jax.random.fold_in(stream_key, axis), (), 0, length) for axis, length in enumerate(values.shape)]
    widest = values.shape.index(max(values.shape))
    next_to = spot[:widest] + [(spot[widest] + 1) % values.shape[widest]] + spot[widest + 1:]
    return values.at[tuple(spot)].set(smallest).at[tuple(next_to)].set(high)


def shard_levels(key, extent, cuts, smallest, largest):
    def one(dim, shards_of):
        steps = jax.random.uniform(jax.random.fold_in(jax.random.fold_in(key, 6), dim), (shards_of,), jnp.float32, smallest / len(cuts), largest / len(cuts))
        return jnp.repeat(jnp.exp(steps), extent[dim] // shards_of).reshape((-1,) + (1,) * (len(extent) - dim - 1))

    gain = one(*cuts[0])
    for cut in cuts[1:]:
        gain = gain * one(*cut)
    return gain


def profile(number_of, total, most, skew):
    portions = [(1 << 20) // math.isqrt(rank ** skew) + 1 for rank in range(2, number_of + 1)]
    spare, holding = total - most - (number_of - 1), [1] * (number_of - 1)
    while spare > 0:
        movable = [i for i in range(number_of - 1) if holding[i] < most]
        whole, budget = sum([portions[i] for i in movable]), spare
        for i in movable:
            addition = min(most - holding[i], max(1, budget * portions[i] // whole), spare)
            holding[i] = holding[i] + addition
            spare = spare - addition
    return np.array([most] + holding)


def ragged(key, amount, total, reach, lean):
    if amount == 2:
        one = jax.random.randint(key, (), max(1, total - reach), min(reach, total - 1) + 1)
        return jnp.stack([one, total - one])
    sizes = jnp.asarray(profile(amount, total, reach, lean), jnp.int32)
    couples = (amount - 1) // 2
    giver, receiver = sizes[1:1 + 2 * couples:2], sizes[2:2 + 2 * couples:2]
    slack = jnp.minimum(giver - 1, reach - receiver)
    passed = jax.random.randint(jax.random.fold_in(key, 1), (couples,), 0, 1 << 20) % (slack + 1)
    sizes = sizes.at[1:1 + 2 * couples:2].set(giver - passed).at[2:2 + 2 * couples:2].set(receiver + passed)
    return sizes[jax.random.permutation(jax.random.fold_in(key, 2), amount)]


def noise(stream_key, extent, deviation, reach, shards=(), held_as=jnp.bfloat16):
    result = jax.random.normal(stream_key, extent, jnp.float32) * deviation
    if len(shards) > 0:
        result = shard_levels(stream_key, extent, shards, -0.22, 0.18) * result
    return jnp.clip(result, min=-reach, max=reach).astype(held_as)


def setup_inputs(seed: int = 0) -> dict:
    streams_of = jax.random.split(jax.random.key(seed), 13)
    activations = noise(streams_of[0], (TOKENS, D), 1.0, 3.0, ((1, 4),))
    cotangent = noise(streams_of[1], (TOKENS, D), 0.1, 0.59765625, ((1, 4),))
    forget = set_ends((jax.random.randint(streams_of[2], (TOKENS,), 0, 4) < 1).astype(jnp.int32), jax.random.fold_in(streams_of[2], 1), 0, 1)
    lengths = jax.vmap(lambda own: ragged(own, SEGS, TOK_BLK, MOST, 1))(jax.random.split(streams_of[3], N_ROW)).reshape((N_ROW, SEGS)).astype(jnp.int32)
    query_weight = noise(streams_of[4], (D, HEADS * HD), D ** -0.5, 0.046875, ((0, 4), (1, 8)))
    key_weight = noise(streams_of[5], (D, KVH * HD), D ** -0.5, 0.046875, ((0, 4),))
    value_weight = noise(streams_of[6], (D, KVH * HD), D ** -0.5, 0.046875, ((0, 4),))
    output_projection_weight = noise(streams_of[7], (HEADS * HD, D), (HEADS * HD) ** -0.5, 0.0625, ((0, 8), (1, 4)))
    query_down = noise(streams_of[8], (D, RANK), D ** -0.5, 0.046875, ((0, 4),))
    query_up = noise(streams_of[9], (RANK, HEADS * HD), RANK ** -0.5, 1.0, ((1, 8),))
    output_down = noise(streams_of[10], (HEADS * HD, RANK), (HEADS * HD) ** -0.5, 0.0625, ((0, 8),))
    output_up = noise(streams_of[11], (RANK, D), RANK ** -0.5, 1.0, ((1, 4),))
    return dict(activations=activations, cotangent=cotangent, forget=forget, lengths=lengths, query_weight=query_weight, key_weight=key_weight, value_weight=value_weight, output_projection_weight=output_projection_weight, query_down=query_down, query_up=query_up, output_down=output_down, output_up=output_up)


adapter_scale = 0.5
highest_precision = lax.Precision.HIGHEST

def to_bf16(value):
    return lax.optimization_barrier(value.astype(jnp.bfloat16))

def rounded_sum(term_fn, shape):

    def add_block(total, block):
        term = to_bf16(term_fn(block))
        return (total + term.astype(jnp.float32), None)
    total, _ = lax.scan(add_block, jnp.zeros(shape, jnp.float32), jnp.arange(N_ROW, dtype=jnp.int32))
    return total

def reference(activations, cotangent, forget, lengths, query_weight, key_weight, value_weight, output_projection_weight, query_down, query_up, output_down, output_up):
    block_width = D // N_ROW
    query_cols = HEADS * HD
    kv_cols = KVH * HD
    group_size = HEADS // KVH
    up_projection_broad = query_up.astype(jnp.float32)
    down_projection_broad = output_down.astype(jnp.float32)
    inverse = 1.0 / math.sqrt(HD)

    def forward_part(block):
        first_col = (block * block_width).astype(jnp.int32)
        inputs = lax.dynamic_slice_in_dim(activations, first_col, block_width, 1)
        reduced_result = jnp.dot(inputs, lax.dynamic_slice_in_dim(query_down, first_col, block_width, 0), preferred_element_type=jnp.float32)
        query_partial_term = jnp.dot(inputs, lax.dynamic_slice_in_dim(query_weight, first_col, block_width, 0), preferred_element_type=jnp.float32)
        query_partial_term = query_partial_term + adapter_scale * jnp.dot(reduced_result, up_projection_broad, precision=highest_precision)
        key_term = jnp.dot(inputs, lax.dynamic_slice_in_dim(key_weight, first_col, block_width, 0), preferred_element_type=jnp.float32)
        value_term = jnp.dot(inputs, lax.dynamic_slice_in_dim(value_weight, first_col, block_width, 0), preferred_element_type=jnp.float32)
        return jnp.concatenate([query_partial_term, key_term, value_term, reduced_result], axis=1)
    summed = rounded_sum(forward_part, (TOKENS, query_cols + 2 * kv_cols + RANK))
    query_rows = to_bf16(summed[:, :query_cols]).astype(jnp.float32)
    key_rows = to_bf16(summed[:, query_cols:query_cols + kv_cols]).astype(jnp.float32)
    value_rows = to_bf16(summed[:, query_cols + kv_cols:query_cols + 2 * kv_cols]).astype(jnp.float32)
    input_lowrank_factor = summed[:, query_cols + 2 * kv_cols:]
    query_heads = query_rows.reshape(N_ROW, TOK_BLK, HEADS, HD)
    key_heads = jnp.repeat(key_rows.reshape(N_ROW, TOK_BLK, KVH, HD), group_size, axis=2)
    value_heads = jnp.repeat(value_rows.reshape(N_ROW, TOK_BLK, KVH, HD), group_size, axis=2)
    seg_ends = jnp.cumsum(lengths, axis=1).astype(jnp.int32)
    position = jnp.arange(TOK_BLK, dtype=jnp.int32)
    segment = lax.optimization_barrier(jnp.sum((position[None, :, None] >= seg_ends[:, None, :]).astype(jnp.int32), axis=2))
    allowed = (segment[:, :, None] == segment[:, None, :]) & (position[None, None, :] <= position[None, :, None])
    scores = jnp.einsum('bqhd,bkhd->bhqk', query_heads, key_heads, precision=highest_precision) * inverse
    numerator = jnp.where(allowed[:, None], jnp.exp(scores), 0.0)
    softmax = numerator / lax.optimization_barrier(jnp.sum(numerator, axis=3, keepdims=True))
    weights = to_bf16(softmax).astype(jnp.float32)
    hidden_state = jnp.einsum('bhqk,bkhd->bqhd', weights, value_heads, precision=highest_precision).reshape(TOKENS, query_cols)
    hidden_state = to_bf16(hidden_state)
    sign_flip = (1 - 2 * forget).astype(jnp.bfloat16)
    output_gradient = cotangent * sign_flip[:, None]

    def backward_part(block):
        first_col = (block * block_width).astype(jnp.int32)
        grads = lax.dynamic_slice_in_dim(output_gradient, first_col, block_width, 1)
        reduced_result = jnp.dot(grads, lax.dynamic_slice_in_dim(output_up, first_col, block_width, 1).T, preferred_element_type=jnp.float32)
        hidden_state_term = jnp.dot(grads, lax.dynamic_slice_in_dim(output_projection_weight, first_col, block_width, 1).T, preferred_element_type=jnp.float32)
        hidden_state_term = hidden_state_term + adapter_scale * jnp.dot(reduced_result, down_projection_broad.T, precision=highest_precision)
        return jnp.concatenate([hidden_state_term, reduced_result], axis=1)
    backward = rounded_sum(backward_part, (TOKENS, query_cols + RANK))
    hidden_grad = to_bf16(backward[:, :query_cols]).astype(jnp.float32).reshape(N_ROW, TOK_BLK, HEADS, HD)
    gradient_lowrank_factor = backward[:, query_cols:]
    prob_grad = jnp.einsum('bqhd,bkhd->bhqk', hidden_grad, value_heads, precision=highest_precision)
    score_grad = softmax * (prob_grad - lax.optimization_barrier(jnp.sum(prob_grad * softmax, axis=3, keepdims=True)))
    query_gradient = (jnp.einsum('bhqk,bkhd->bqhd', score_grad, key_heads, precision=highest_precision) * inverse).reshape(TOKENS, query_cols)
    query_lowrank_factor = to_bf16(jnp.dot(query_gradient, up_projection_broad.T, precision=highest_precision))
    hidden_state_factor = to_bf16(jnp.dot(hidden_state, output_down, preferred_element_type=jnp.float32))
    contraction_rows = (((0,), (0,)), ((), ()))
    query_down_gradient = adapter_scale * lax.dot_general(activations, query_lowrank_factor, contraction_rows, preferred_element_type=jnp.float32)
    query_up_gradient = adapter_scale * jnp.dot(input_lowrank_factor.T, query_gradient, precision=highest_precision)
    output_down_gradient = adapter_scale * jnp.dot(hidden_state.astype(jnp.float32).T, gradient_lowrank_factor, precision=highest_precision)
    output_up_gradient = adapter_scale * lax.dot_general(hidden_state_factor, output_gradient, contraction_rows, preferred_element_type=jnp.float32)
    return (query_down_gradient, query_up_gradient, output_down_gradient, output_up_gradient)
```

```python
import functools
import math

import jax
import jax.numpy as jnp
from jax import lax
from jax.experimental import pallas as pl
from jax.experimental.pallas import tpu as pltpu
from jax.sharding import PartitionSpec as P

HD = 128
HEADS = 64
KVH = 4

SCALE = 0.5
BF = jnp.bfloat16
F32 = jnp.float32


def mm(left, right, a, b):
    return lax.dot_general(
        left, right, (((a,), (b,)), ((), ())), preferred_element_type=F32
    )


def kernel(
    n_row,
    n_col,
    lengths_ref,
    forget_ref,
    x_hbm,
    cot_hbm,
    wq_hbm,
    wk_hbm,
    wv_hbm,
    wo_hbm,
    qd_hbm,
    up_hbm,
    od_hbm,
    ou_hbm,
    dq_ref,
    pieces_ref,
    du_ref,
    x,
    cot,
    wq,
    wkv,
    wo,
    qd,
    up,
    od,
    ou,
    red,
    chunk_send,
    chunk_recv,
    small_send,
    small_recv,
    fac_send,
    fac_recv,
    fac_all,
    piece_send,
    piece_recv,
    piece_all,
    load_sem,
    wq_sem,
    wo_sem,
    chunk_ss,
    chunk_rs,
    small_ss,
    small_rs,
    fac_ss,
    fac_rs,
    all_ss,
    all_rs,
    piece_ss,
    piece_rs,
    gat_ss,
    gat_rs,
):
    me = lax.axis_index("row")
    mc = lax.axis_index("col")
    n_chunk, depth, width = wq.shape
    rank = qd.shape[1]
    tokens = x.shape[0]
    blk = tokens // n_row
    heads = n_chunk * width // HD
    per = width // HD
    inverse = 1.0 / math.sqrt(HD)
    group = lax.div(mc * heads, HEADS // KVH)
    group_cols = pl.ds(pl.multiple_of(group * HD, HD), HD)

    def row_peer(d):
        return lax.rem(me + d, n_row)

    def col_peer(d):
        return lax.rem(mc + d, n_col)

    def load_wq(c):
        return pltpu.make_async_copy(
            wq_hbm.at[:, pl.ds(c * width, width)], wq.at[c], wq_sem.at[c]
        )

    def load_wo(c):
        return pltpu.make_async_copy(
            wo_hbm.at[pl.ds(c * width, width), :], wo.at[c], wo_sem.at[c]
        )

    def up_load(c):
        return pltpu.make_async_copy(
            up_hbm.at[:, pl.ds(c * width, width)], up.at[c], load_sem.at[7 + c]
        )

    load_x = pltpu.make_async_copy(x_hbm, x, load_sem.at[0])
    load_qd = pltpu.make_async_copy(qd_hbm, qd, load_sem.at[1])
    load_k = pltpu.make_async_copy(wk_hbm.at[:, group_cols], wkv.at[0], load_sem.at[2])
    load_v = pltpu.make_async_copy(wv_hbm.at[:, group_cols], wkv.at[1], load_sem.at[3])
    load_cot = pltpu.make_async_copy(cot_hbm, cot, load_sem.at[4])
    load_ou = pltpu.make_async_copy(ou_hbm, ou, load_sem.at[5])
    load_od = pltpu.make_async_copy(od_hbm, od, load_sem.at[6])
    load_x.start()
    load_qd.start()
    for c in range(n_chunk):
        up_load(c).start()
    for c in range(n_chunk):
        load_wq(c).start()
    load_k.start()
    load_v.start()
    load_cot.start()
    load_ou.start()
    load_od.start()
    for c in range(n_chunk):
        load_wo(c).start()

    barrier = pltpu.get_barrier_semaphore()
    for d in range(1, n_row):
        pl.semaphore_signal(
            barrier, inc=1, device_id={"row": row_peer(d)}, device_id_type=pl.DeviceIdType.MESH
        )
    for d in range(1, n_col):
        pl.semaphore_signal(
            barrier, inc=1, device_id={"col": col_peer(d)}, device_id_type=pl.DeviceIdType.MESH
        )

    def remote(src, dst, send, recv, where):
        return pltpu.make_async_remote_copy(
            src_ref=src,
            dst_ref=dst,
            send_sem=send,
            recv_sem=recv,
            device_id=where,
            device_id_type=pl.DeviceIdType.MESH,
        )

    def chunk_copy(c, d):
        p = row_peer(d)
        return remote(
            chunk_send.at[c, p], chunk_recv.at[c, d], chunk_ss.at[c, d], chunk_rs.at[c, d], {"row": p}
        )

    def small_copy(d):
        p = row_peer(d)
        return remote(small_send.at[p], small_recv.at[d], small_ss.at[d], small_rs.at[d], {"row": p})

    def fac_copy(d):
        return remote(fac_send, fac_recv.at[d], fac_ss.at[d], fac_rs.at[d], {"col": col_peer(d)})

    def all_copy(d):
        return remote(
            fac_all.at[me], fac_all.at[me], all_ss.at[d], all_rs.at[d], {"row": row_peer(d)}
        )

    def all_arrival(d):
        return remote(
            fac_all.at[me], fac_all.at[row_peer(n_row - d)], all_ss.at[d], all_rs.at[d], {"row": row_peer(d)}
        )

    def piece_copy(d):
        p = row_peer(d)
        return remote(piece_send.at[p], piece_recv.at[d], piece_ss.at[d], piece_rs.at[d], {"row": p})

    def gat_copy(d):
        return remote(
            piece_all.at[me], piece_all.at[me], gat_ss.at[d], gat_rs.at[d], {"row": row_peer(d)}
        )

    def gat_arrival(d):
        return remote(
            piece_all.at[me], piece_all.at[row_peer(n_row - d)], gat_ss.at[d], gat_rs.at[d], {"row": row_peer(d)}
        )

    load_x.wait()
    load_qd.wait()
    for c in range(n_chunk):
        up_load(c).wait()
    lowrank = mm(x[...], qd[...], 1, 0)
    red[0] = lowrank.astype(BF)
    pl.semaphore_wait(barrier, n_row + n_col - 2)

    @pl.loop(0, n_chunk)
    def _(c):
        pltpu.make_async_copy(
            wq_hbm.at[:, pl.ds(0, width)], wq.at[c], wq_sem.at[c]
        ).wait()
        term = mm(x[...], wq[c], 1, 0) + SCALE * mm(red[0], up[c], 1, 0)
        chunk_send[c] = term.astype(BF).reshape(n_row, blk, width)
        for d in range(1, n_row):
            chunk_copy(c, d).start()

    load_k.wait()
    load_v.wait()
    small_send[:, :, 0:HD] = mm(x[...], wkv[0], 1, 0).astype(BF).reshape(n_row, blk, HD)
    small_send[:, :, HD : 2 * HD] = mm(x[...], wkv[1], 1, 0).astype(BF).reshape(n_row, blk, HD)
    load_cot.wait()
    load_ou.wait()
    load_od.wait()
    red[1] = mm(cot[...], ou[...], 1, 1).astype(BF)
    small_send[:, :, 2 * HD :] = jnp.concatenate(
        [red[0], red[1], jnp.zeros((tokens, HD - 2 * rank), BF)], axis=1
    ).reshape(n_row, blk, HD)
    for d in range(1, n_row):
        small_copy(d).start()

    @pl.loop(0, n_chunk)
    def _(c):
        pltpu.make_async_copy(
            wo_hbm.at[pl.ds(0, width), :], wo.at[c], wo_sem.at[c]
        ).wait()
        down = od[pl.ds(pl.multiple_of(c * width, width), width), :]
        term = mm(cot[...], wo[c], 1, 1) + SCALE * mm(red[1], down, 1, 1)
        chunk_send[n_chunk + c] = term.astype(BF).reshape(n_row, blk, width)
        for d in range(1, n_row):
            chunk_copy(n_chunk + c, d).start()

    def chunk_sum(c):
        total = chunk_send[c, me].astype(F32)
        for d in range(1, n_row):
            chunk_copy(c, d).wait_recv()
            total = total + chunk_recv[c, d].astype(F32)
        return total

    def sign_of(first):
        lane = lax.broadcasted_iota(jnp.int32, (blk, tokens), 1)
        sub = lax.broadcasted_iota(jnp.int32, (blk, tokens), 0)
        picked = jnp.where(lane == sub + first, forget_ref[...], 0)
        return (1 - 2 * jnp.sum(picked, axis=1, keepdims=True)).astype(F32)

    sign = sign_of(me * blk)

    stacked = []
    for c in range(n_chunk):
        part = chunk_sum(c).astype(BF)
        for h in range(per):
            stacked.append(part[:, h * HD : (h + 1) * HD])
    query = jnp.concatenate(stacked, axis=0)
    small = small_send[me].astype(F32)
    for d in range(1, n_row):
        small_copy(d).wait_recv()
        small = small + small_recv[d].astype(F32)
    key = small[:, 0:HD].astype(BF)
    value = small[:, HD : 2 * HD].astype(BF)
    in_low = small[:, 2 * HD : 2 * HD + rank].astype(BF)
    grad_low = (small[:, 2 * HD + rank : 2 * HD + 2 * rank] * sign).astype(BF)

    rows = heads * blk
    pos_q = lax.rem(lax.broadcasted_iota(jnp.int32, (rows, blk), 0), blk)
    pos_k = lax.broadcasted_iota(jnp.int32, (rows, blk), 1)
    seg_q = jnp.zeros((rows, blk), jnp.int32)
    seg_k = jnp.zeros((rows, blk), jnp.int32)
    end = 0
    for i in range(lengths_ref.shape[1]):
        end = end + lengths_ref[0, i]
        seg_q = seg_q + (pos_q >= end).astype(jnp.int32)
        seg_k = seg_k + (pos_k >= end).astype(jnp.int32)
    allowed = (seg_q == seg_k) & (pos_k <= pos_q)
    scores = mm(query, key, 1, 1) * inverse
    numer = jnp.where(allowed, jnp.exp(scores), 0.0)
    softmax = numer / jnp.sum(numer, axis=1, keepdims=True)
    hidden = mm(softmax.astype(BF), value, 1, 0).astype(BF)
    hidden_flat = jnp.concatenate([hidden[h * blk : (h + 1) * blk] for h in range(heads)], axis=1)
    hidden_factor = mm(hidden_flat, od[...], 1, 0)
    down_piece = SCALE * mm(grad_low, hidden_flat, 0, 0)

    stacked = []
    for c in range(n_chunk):
        part = (chunk_sum(n_chunk + c) * sign).astype(BF)
        for h in range(per):
            stacked.append(part[:, h * HD : (h + 1) * HD])
    hidden_grad = jnp.concatenate(stacked, axis=0)
    prob_grad = mm(hidden_grad, value, 1, 1)
    score_grad = softmax * (prob_grad - jnp.sum(prob_grad * softmax, axis=1, keepdims=True))
    query_grad = (mm(score_grad.astype(BF), key, 1, 0) * inverse).astype(BF)
    grad_flat = jnp.concatenate(
        [query_grad[h * blk : (h + 1) * blk] for h in range(heads)], axis=1
    )
    query_factor = mm(grad_flat[:, 0:width], up[0], 1, 1)
    for c in range(1, n_chunk):
        query_factor = query_factor + mm(grad_flat[:, c * width : (c + 1) * width], up[c], 1, 1)
    factors = jnp.concatenate([query_factor, hidden_factor], axis=1)
    half = blk // 2
    packed = jnp.concatenate([factors[:half], factors[half:]], axis=1)
    fac_send[...] = packed.astype(BF)
    for d in range(1, n_col):
        fac_copy(d).start()
    up_piece = SCALE * mm(in_low, grad_flat, 0, 0)
    both = jnp.concatenate([up_piece, down_piece], axis=0).astype(BF)
    share = piece_send.shape[1]
    for r in range(n_row):
        piece_send[r] = both[r * share : (r + 1) * share]
    for d in range(1, n_row):
        piece_copy(d).start()

    total = fac_send[...].astype(F32)
    for d in range(1, n_col):
        fac_copy(d).wait_recv()
        total = total + fac_recv[d].astype(F32)
    fac_all[me] = total.astype(BF)
    for d in range(1, n_row):
        all_copy(d).start()
    total = piece_send[me].astype(F32)
    for d in range(1, n_row):
        piece_copy(d).wait_recv()
        total = total + piece_recv[d].astype(F32)
    piece_all[me] = total.astype(BF)
    for d in range(1, n_row):
        gat_copy(d).start()

    for d in range(1, n_row):
        all_arrival(d).wait_recv()
    query_all, hidden_all = [], []
    for r in range(n_row):
        block = fac_all[r].astype(F32)
        block = jnp.concatenate([block[:, : 2 * rank], block[:, 2 * rank : 4 * rank]], axis=0)
        query_all.append(block[:, :rank].astype(BF))
        hidden_all.append((block[:, rank : 2 * rank] * sign_of(r * blk)).astype(BF))
    dq_ref[...] = SCALE * mm(jnp.concatenate(query_all, axis=0), x[...], 0, 0)
    du_ref[...] = SCALE * mm(jnp.concatenate(hidden_all, axis=0), cot[...], 0, 0)
    for d in range(1, n_row):
        gat_arrival(d).wait_recv()
    for r in range(n_row):
        pieces_ref[r * share : (r + 1) * share, :] = piece_all[r].astype(F32)

    for d in range(1, n_row):
        for c in range(2 * n_chunk):
            chunk_copy(c, d).wait_send()
        small_copy(d).wait_send()
        all_copy(d).wait_send()
        piece_copy(d).wait_send()
        gat_copy(d).wait_send()
    for d in range(1, n_col):
        fac_copy(d).wait_send()


def local(
    activations,
    cotangent,
    forget,
    lengths,
    query_weight,
    key_weight,
    value_weight,
    output_projection_weight,
    query_down,
    query_up,
    output_down,
    output_up,
):
    n_row, n_col = lax.axis_size("row"), lax.axis_size("col")
    tokens, depth = activations.shape
    cols = query_weight.shape[1]
    rank = query_down.shape[1]
    blk = tokens // n_row
    width = min(256, cols)
    n_chunk = cols // width
    share = 2 * rank // n_row
    any_spec = pl.BlockSpec(memory_space=pl.ANY)
    vmem = pl.BlockSpec(memory_space=pltpu.VMEM)
    dma = pltpu.SemaphoreType.DMA
    dq, pieces, du = pl.pallas_call(
        functools.partial(kernel, n_row, n_col),
        out_shape=(
            jax.ShapeDtypeStruct((rank, depth), F32),
            jax.ShapeDtypeStruct((2 * rank, cols), F32),
            jax.ShapeDtypeStruct((rank, depth), F32),
        ),
        in_specs=[pl.BlockSpec(memory_space=pltpu.SMEM), vmem] + [any_spec] * 10,
        out_specs=(vmem, vmem, vmem),
        scratch_shapes=[
            pltpu.VMEM((tokens, depth), BF),
            pltpu.VMEM((tokens, depth), BF),
            pltpu.VMEM((n_chunk, depth, width), BF),
            pltpu.VMEM((2, depth, HD), BF),
            pltpu.VMEM((n_chunk, width, depth), BF),
            pltpu.VMEM((depth, rank), BF),
            pltpu.VMEM((n_chunk, rank, width), BF),
            pltpu.VMEM((cols, rank), BF),
            pltpu.VMEM((rank, depth), BF),
            pltpu.VMEM((2, tokens, rank), BF),
            pltpu.VMEM((2 * n_chunk, n_row, blk, width), BF),
            pltpu.VMEM((2 * n_chunk, n_row, blk, width), BF),
            pltpu.VMEM((n_row, blk, 3 * HD), BF),
            pltpu.VMEM((n_row, blk, 3 * HD), BF),
            pltpu.VMEM((blk // 2, 4 * rank), BF),
            pltpu.VMEM((n_col, blk // 2, 4 * rank), BF),
            pltpu.VMEM((n_row, blk // 2, 4 * rank), BF),
            pltpu.VMEM((n_row, share, cols), BF),
            pltpu.VMEM((n_row, share, cols), BF),
            pltpu.VMEM((n_row, share, cols), BF),
            dma((7 + n_chunk,)),
            dma((n_chunk,)),
            dma((n_chunk,)),
            dma((2 * n_chunk, n_row)),
            dma((2 * n_chunk, n_row)),
            dma((n_row,)),
            dma((n_row,)),
            dma((n_col,)),
            dma((n_col,)),
            dma((n_row,)),
            dma((n_row,)),
            dma((n_row,)),
            dma((n_row,)),
            dma((n_row,)),
            dma((n_row,)),
        ],
        compiler_params=pltpu.CompilerParams(
            collective_id=0, has_side_effects=True, vmem_limit_bytes=50 << 20
        ),
        name="unlearn_step",
    )(
        lengths,
        forget.reshape(1, tokens),
        activations,
        cotangent,
        query_weight,
        key_weight,
        value_weight,
        output_projection_weight,
        query_down,
        query_up,
        output_down,
        output_up,
    )
    return dq.T, pieces[:rank], pieces[rank:].T, du


def solution(mesh):
    placed = (
        P(None, "row"),
        P(None, "row"),
        P(),
        P("row", None),
        P("row", "col"),
        P("row", None),
        P("row", None),
        P("col", "row"),
        P("row", None),
        P(None, "col"),
        P("col", None),
        P(None, "row"),
    )
    return jax.shard_map(
        local,
        mesh=mesh,
        in_specs=placed,
        out_specs=(P("row", None), P(None, "col"), P("col", None), P(None, "row")),
        check_vma=False,
    )
```

```python
import functools
import math

import jax
import jax.numpy as jnp
from jax import lax
from jax.experimental import pallas as pl
from jax.experimental.pallas import tpu as pltpu
from jax.sharding import PartitionSpec as P

HD = 128
HEADS = 64
KVH = 4

SCALE = 0.5
BF = jnp.bfloat16
F32 = jnp.float32


def mm(left, right, a, b):
    return lax.dot_general(
        left, right, (((a,), (b,)), ((), ())), preferred_element_type=F32
    )


def kernel(
    n_row,
    n_col,
    lengths_hbm,
    forget_hbm,
    x_hbm,
    cot_hbm,
    wq_hbm,
    wk_hbm,
    wv_hbm,
    wo_hbm,
    qd_hbm,
    up_hbm,
    od_hbm,
    ou_hbm,
    dq_ref,
    pieces_ref,
    du_ref,
    x,
    cot,
    wq,
    wkv,
    wo,
    qd,
    up,
    od,
    ou,
    red,
    chunk_send,
    chunk_recv,
    small_send,
    small_recv,
    fac_send,
    fac_recv,
    fac_all,
    piece_send,
    piece_recv,
    piece_all,
    lengths_ref,
    forget_ref,
    load_sem,
    wq_sem,
    wo_sem,
    chunk_ss,
    chunk_rs,
    small_ss,
    small_rs,
    fac_ss,
    fac_rs,
    all_ss,
    all_rs,
    piece_ss,
    piece_rs,
    gat_ss,
    gat_rs,
):
    me = lax.axis_index("row")
    mc = lax.axis_index("col")
    n_chunk, depth, width = wq.shape
    rank = qd.shape[0]
    tokens = x.shape[0]
    blk = tokens // n_row
    heads = n_chunk * width // HD
    per = width // HD
    inverse = 1.0 / math.sqrt(HD)
    group = lax.div(mc * heads, HEADS // KVH)
    group_cols = pl.ds(pl.multiple_of(group * HD, HD), HD)

    def row_peer(d):
        return lax.rem(me + d, n_row)

    def col_peer(d):
        return lax.rem(mc + d, n_col)

    def load_wq(c):
        return pltpu.make_async_copy(
            wq_hbm.at[:, pl.ds(c * width, width)], wq.at[c], wq_sem.at[c]
        )

    def load_wo(c):
        return pltpu.make_async_copy(
            wo_hbm.at[pl.ds(c * width, width), :], wo.at[c], wo_sem.at[c]
        )

    def up_load(c):
        return pltpu.make_async_copy(
            up_hbm.at[:, pl.ds(c * width, width)], up.at[c], load_sem.at[8 + c]
        )

    def od_load(c):
        return pltpu.make_async_copy(
            od_hbm.at[:, pl.ds(c * width, width)], od.at[c], load_sem.at[8 + n_chunk + c]
        )

    load_x = pltpu.make_async_copy(x_hbm, x, load_sem.at[0])
    load_qd = pltpu.make_async_copy(qd_hbm, qd, load_sem.at[1])
    load_k = pltpu.make_async_copy(wk_hbm.at[:, group_cols], wkv.at[0], load_sem.at[2])
    load_v = pltpu.make_async_copy(wv_hbm.at[:, group_cols], wkv.at[1], load_sem.at[3])
    load_cot = pltpu.make_async_copy(cot_hbm, cot, load_sem.at[4])
    load_ou = pltpu.make_async_copy(ou_hbm, ou, load_sem.at[5])
    load_len = pltpu.make_async_copy(lengths_hbm, lengths_ref, load_sem.at[6])
    load_forget = pltpu.make_async_copy(forget_hbm, forget_ref, load_sem.at[7])
    load_x.start()
    load_qd.start()
    for c in range(n_chunk):
        up_load(c).start()
    for c in range(n_chunk):
        load_wq(c).start()
    load_k.start()
    load_v.start()
    load_cot.start()
    load_ou.start()
    for c in range(n_chunk):
        od_load(c).start()
    load_len.start()
    load_forget.start()
    for c in range(n_chunk):
        load_wo(c).start()

    barrier = pltpu.get_barrier_semaphore()
    for d in range(1, n_row):
        pl.semaphore_signal(
            barrier, inc=1, device_id={"row": row_peer(d)}, device_id_type=pl.DeviceIdType.MESH
        )
    for d in range(1, n_col):
        pl.semaphore_signal(
            barrier, inc=1, device_id={"col": col_peer(d)}, device_id_type=pl.DeviceIdType.MESH
        )

    def remote(src, dst, send, recv, where):
        return pltpu.make_async_remote_copy(
            src_ref=src,
            dst_ref=dst,
            send_sem=send,
            recv_sem=recv,
            device_id=where,
            device_id_type=pl.DeviceIdType.MESH,
        )

    def chunk_copy(c, d):
        p = row_peer(d)
        return remote(
            chunk_send.at[c, p], chunk_recv.at[c, d], chunk_ss.at[c, d], chunk_rs.at[c, d], {"row": p}
        )

    def small_copy(d):
        p = row_peer(d)
        return remote(small_send.at[p], small_recv.at[d], small_ss.at[d], small_rs.at[d], {"row": p})

    def fac_copy(j, d):
        return remote(
            fac_send.at[j], fac_recv.at[j, d], fac_ss.at[j, d], fac_rs.at[j, d], {"col": col_peer(d)}
        )

    def all_copy(j, d, owner):
        return remote(
            fac_all.at[j, me], fac_all.at[j, owner], all_ss.at[j, d], all_rs.at[j, d], {"row": row_peer(d)}
        )

    def piece_copy(j, d):
        p = row_peer(d)
        return remote(
            piece_send.at[j, p], piece_recv.at[j, d], piece_ss.at[j, d], piece_rs.at[j, d], {"row": p}
        )

    def gat_copy(j, d, owner):
        return remote(
            piece_all.at[j, me], piece_all.at[j, owner], gat_ss.at[j, d], gat_rs.at[j, d], {"row": row_peer(d)}
        )

    quarter = blk // 4
    share = piece_send.shape[2]

    def send_factor(j, factor):
        packed = jnp.concatenate(
            [factor[i * quarter : (i + 1) * quarter] for i in range(4)], axis=1
        )
        fac_send[j] = packed.astype(BF)
        for d in range(1, n_col):
            fac_copy(j, d).start()

    def spread_factor(j):
        total = fac_send[j].astype(F32)
        for d in range(1, n_col):
            fac_copy(j, d).wait_recv()
            total = total + fac_recv[j, d].astype(F32)
        fac_all[j, me] = total.astype(BF)
        for d in range(1, n_row):
            all_copy(j, d, me).start()

    def factor_everywhere(j):
        for d in range(1, n_row):
            all_copy(j, d, row_peer(n_row - d)).wait_recv()
        blocks = []
        for r in range(n_row):
            block = fac_all[j, r].astype(F32)
            blocks.append(
                jnp.concatenate([block[:, i * rank : (i + 1) * rank] for i in range(4)], axis=0)
            )
        return blocks

    def send_piece(j, piece):
        for r in range(n_row):
            piece_send[j, r] = piece[r * share : (r + 1) * share].astype(BF)
        for d in range(1, n_row):
            piece_copy(j, d).start()

    def spread_piece(j):
        total = piece_send[j, me].astype(F32)
        for d in range(1, n_row):
            piece_copy(j, d).wait_recv()
            total = total + piece_recv[j, d].astype(F32)
        piece_all[j, me] = total.astype(BF)
        for d in range(1, n_row):
            gat_copy(j, d, me).start()

    def finish_piece(j):
        for d in range(1, n_row):
            gat_copy(j, d, row_peer(n_row - d)).wait_recv()
        for r in range(n_row):
            first = j * rank + r * share
            pieces_ref[first : first + share, :] = piece_all[j, r].astype(F32)

    load_x.wait()
    load_qd.wait()
    for c in range(n_chunk):
        up_load(c).wait()
    lowrank = mm(x[...], qd[...], 1, 1)
    red[0] = lowrank.astype(BF)
    pl.semaphore_wait(barrier, n_row + n_col - 2)

    @pl.loop(0, n_chunk)
    def _(c):
        pltpu.make_async_copy(
            wq_hbm.at[:, pl.ds(0, width)], wq.at[c], wq_sem.at[c]
        ).wait()
        term = mm(x[...], wq[c], 1, 0) + SCALE * mm(red[0], up[c], 1, 0)
        chunk_send[c] = term.astype(BF).reshape(n_row, blk, width)
        for d in range(1, n_row):
            chunk_copy(c, d).start()

    load_k.wait()
    load_v.wait()
    small_send[:, :, 0:HD] = mm(x[...], wkv[0], 1, 0).astype(BF).reshape(n_row, blk, HD)
    small_send[:, :, HD : 2 * HD] = mm(x[...], wkv[1], 1, 0).astype(BF).reshape(n_row, blk, HD)
    load_cot.wait()
    load_ou.wait()
    for c in range(n_chunk):
        od_load(c).wait()
    red[1] = mm(cot[...], ou[...], 1, 1).astype(BF)
    small_send[:, :, 2 * HD :] = jnp.concatenate(
        [red[0], red[1], jnp.zeros((tokens, HD - 2 * rank), BF)], axis=1
    ).reshape(n_row, blk, HD)
    for d in range(1, n_row):
        small_copy(d).start()

    @pl.loop(0, n_chunk)
    def _(c):
        pltpu.make_async_copy(
            wo_hbm.at[pl.ds(0, width), :], wo.at[c], wo_sem.at[c]
        ).wait()
        term = mm(cot[...], wo[c], 1, 1) + SCALE * mm(red[1], od[c], 1, 0)
        chunk_send[n_chunk + c] = term.astype(BF).reshape(n_row, blk, width)
        for d in range(1, n_row):
            chunk_copy(n_chunk + c, d).start()

    def chunk_sum(c):
        total = chunk_send[c, me].astype(F32)
        for d in range(1, n_row):
            chunk_copy(c, d).wait_recv()
            total = total + chunk_recv[c, d].astype(F32)
        return total

    def sign_of(first):
        lane = lax.broadcasted_iota(jnp.int32, (blk, tokens), 1)
        sub = lax.broadcasted_iota(jnp.int32, (blk, tokens), 0)
        picked = jnp.where(lane == sub + first, forget_ref[...], 0)
        return (1 - 2 * jnp.sum(picked, axis=1, keepdims=True)).astype(F32)

    load_len.wait()
    load_forget.wait()
    sign = sign_of(me * blk)

    stacked = []
    for c in range(n_chunk):
        part = chunk_sum(c).astype(BF)
        for h in range(per):
            stacked.append(part[:, h * HD : (h + 1) * HD])
    query = jnp.concatenate(stacked, axis=0)
    small = small_send[me].astype(F32)
    for d in range(1, n_row):
        small_copy(d).wait_recv()
        small = small + small_recv[d].astype(F32)
    key = small[:, 0:HD].astype(BF)
    value = small[:, HD : 2 * HD].astype(BF)
    in_low = small[:, 2 * HD : 2 * HD + rank].astype(BF)
    grad_low = (small[:, 2 * HD + rank : 2 * HD + 2 * rank] * sign).astype(BF)

    rows = heads * blk
    pos_q = lax.rem(lax.broadcasted_iota(jnp.int32, (rows, blk), 0), blk)
    pos_k = lax.broadcasted_iota(jnp.int32, (rows, blk), 1)
    seg_q = jnp.zeros((rows, blk), jnp.int32)
    seg_k = jnp.zeros((rows, blk), jnp.int32)
    end = 0
    for i in range(lengths_ref.shape[1]):
        end = end + lengths_ref[0, i]
        seg_q = seg_q + (pos_q >= end).astype(jnp.int32)
        seg_k = seg_k + (pos_k >= end).astype(jnp.int32)
    allowed = (seg_q == seg_k) & (pos_k <= pos_q)
    scores = mm(query, key, 1, 1) * inverse
    numer = jnp.where(allowed, jnp.exp(scores), 0.0)
    softmax = numer / jnp.sum(numer, axis=1, keepdims=True)
    hidden = mm(softmax.astype(BF), value, 1, 0).astype(BF)
    hidden_flat = jnp.concatenate([hidden[h * blk : (h + 1) * blk] for h in range(heads)], axis=1)
    hidden_factor = mm(hidden_flat[:, 0:width], od[0], 1, 1)
    for c in range(1, n_chunk):
        hidden_factor = hidden_factor + mm(hidden_flat[:, c * width : (c + 1) * width], od[c], 1, 1)
    send_factor(1, hidden_factor)
    send_piece(1, SCALE * mm(grad_low, hidden_flat, 0, 0))
    signs = [sign_of(r * blk) for r in range(n_row)]
    spread_factor(1)

    query_factor = jnp.zeros((blk, rank), F32)
    up_parts = []
    span = per * blk
    for c in range(n_chunk):
        part = (chunk_sum(n_chunk + c) * sign).astype(BF)
        hidden_grad = jnp.concatenate([part[:, h * HD : (h + 1) * HD] for h in range(per)], axis=0)
        soft = softmax[c * span : (c + 1) * span]
        prob_grad = mm(hidden_grad, value, 1, 1)
        score_grad = soft * (prob_grad - jnp.sum(prob_grad * soft, axis=1, keepdims=True))
        query_grad = (mm(score_grad.astype(BF), key, 1, 0) * inverse).astype(BF)
        flat = jnp.concatenate([query_grad[h * blk : (h + 1) * blk] for h in range(per)], axis=1)
        query_factor = query_factor + mm(flat, up[c], 1, 1)
        up_parts.append(SCALE * mm(in_low, flat, 0, 0))
    send_factor(0, query_factor)
    send_piece(0, jnp.concatenate(up_parts, axis=1))

    spread_piece(1)
    blocks = [(b * s).astype(BF) for b, s in zip(factor_everywhere(1), signs)]
    du_ref[...] = SCALE * mm(jnp.concatenate(blocks, axis=0), cot[...], 0, 0)
    spread_factor(0)
    spread_piece(0)
    blocks = [b.astype(BF) for b in factor_everywhere(0)]
    dq_ref[...] = SCALE * mm(jnp.concatenate(blocks, axis=0), x[...], 0, 0)
    finish_piece(1)
    finish_piece(0)

    for d in range(1, n_row):
        for c in range(2 * n_chunk):
            chunk_copy(c, d).wait_send()
        small_copy(d).wait_send()
        for j in range(2):
            all_copy(j, d, me).wait_send()
            piece_copy(j, d).wait_send()
            gat_copy(j, d, me).wait_send()
    for d in range(1, n_col):
        for j in range(2):
            fac_copy(j, d).wait_send()


def writer(dq, pieces, du, o_qd, o_up, o_od, o_ou, sem):
    rank = dq.shape[0]
    moves = [
        pltpu.make_async_copy(dq, o_qd, sem.at[0]),
        pltpu.make_async_copy(du, o_ou, sem.at[1]),
        pltpu.make_async_copy(pieces.at[pl.ds(0, rank)], o_up, sem.at[2]),
        pltpu.make_async_copy(pieces.at[pl.ds(rank, rank)], o_od, sem.at[3]),
    ]
    for move in moves:
        move.start()
    for move in moves:
        move.wait()


def local(
    activations,
    cotangent,
    forget,
    lengths,
    query_weight,
    key_weight,
    value_weight,
    output_projection_weight,
    query_down,
    query_up,
    output_down,
    output_up,
):
    n_row, n_col = lax.axis_size("row"), lax.axis_size("col")
    tokens, depth = activations.shape
    cols = query_weight.shape[1]
    rank = query_down.shape[1]
    blk = tokens // n_row
    width = min(256, cols)
    n_chunk = cols // width
    share = rank // n_row
    hbm = pl.BlockSpec(memory_space=pltpu.HBM)
    vmem = pl.BlockSpec(memory_space=pltpu.VMEM)
    dma = pltpu.SemaphoreType.DMA
    dq, pieces, du = pl.pallas_call(
        functools.partial(kernel, n_row, n_col),
        out_shape=(
            jax.ShapeDtypeStruct((rank, depth), F32),
            jax.ShapeDtypeStruct((2 * rank, cols), F32),
            jax.ShapeDtypeStruct((rank, depth), F32),
        ),
        in_specs=[hbm] * 12,
        out_specs=(vmem, vmem, vmem),
        scratch_shapes=[
            pltpu.VMEM((tokens, depth), BF),
            pltpu.VMEM((tokens, depth), BF),
            pltpu.VMEM((n_chunk, depth, width), BF),
            pltpu.VMEM((2, depth, HD), BF),
            pltpu.VMEM((n_chunk, width, depth), BF),
            pltpu.VMEM((rank, depth), BF),
            pltpu.VMEM((n_chunk, rank, width), BF),
            pltpu.VMEM((n_chunk, rank, width), BF),
            pltpu.VMEM((rank, depth), BF),
            pltpu.VMEM((2, tokens, rank), BF),
            pltpu.VMEM((2 * n_chunk, n_row, blk, width), BF),
            pltpu.VMEM((2 * n_chunk, n_row, blk, width), BF),
            pltpu.VMEM((n_row, blk, 3 * HD), BF),
            pltpu.VMEM((n_row, blk, 3 * HD), BF),
            pltpu.VMEM((2, blk // 4, 4 * rank), BF),
            pltpu.VMEM((2, n_col, blk // 4, 4 * rank), BF),
            pltpu.VMEM((2, n_row, blk // 4, 4 * rank), BF),
            pltpu.VMEM((2, n_row, share, cols), BF),
            pltpu.VMEM((2, n_row, share, cols), BF),
            pltpu.VMEM((2, n_row, share, cols), BF),
            pltpu.SMEM(lengths.shape, jnp.int32),
            pltpu.VMEM((1, tokens), jnp.int32),
            dma((8 + 2 * n_chunk,)),
            dma((n_chunk,)),
            dma((n_chunk,)),
            dma((2 * n_chunk, n_row)),
            dma((2 * n_chunk, n_row)),
            dma((n_row,)),
            dma((n_row,)),
            dma((2, n_col)),
            dma((2, n_col)),
            dma((2, n_row)),
            dma((2, n_row)),
            dma((2, n_row)),
            dma((2, n_row)),
            dma((2, n_row)),
            dma((2, n_row)),
        ],
        compiler_params=pltpu.CompilerParams(
            collective_id=0, has_side_effects=True, vmem_limit_bytes=50 << 20
        ),
        name="unlearn_step",
    )(
        *(
            pltpu.with_memory_space_constraint(operand, pltpu.HBM)
            for operand in (
                lengths,
                forget.reshape(1, tokens),
                activations,
                cotangent,
                query_weight,
                key_weight,
                value_weight,
                output_projection_weight,
                query_down.T,
                query_up,
                output_down.T,
                output_up,
            )
        )
    )
    down_grad, up_grad, out_down_grad, out_up_grad = pl.pallas_call(
        writer,
        out_shape=(
            jax.ShapeDtypeStruct((rank, depth), F32),
            jax.ShapeDtypeStruct((rank, cols), F32),
            jax.ShapeDtypeStruct((rank, cols), F32),
            jax.ShapeDtypeStruct((rank, depth), F32),
        ),
        in_specs=[pl.BlockSpec(memory_space=pl.ANY)] * 3,
        out_specs=(hbm,) * 4,
        scratch_shapes=[dma((4,))],
        compiler_params=pltpu.CompilerParams(vmem_limit_bytes=1 << 20),
        name="write_outputs",
    )(dq, pieces, du)
    return down_grad.T, up_grad, out_down_grad.T, out_up_grad


def solution(mesh):
    placed = (
        P(None, "row"),
        P(None, "row"),
        P(),
        P("row", None),
        P("row", "col"),
        P("row", None),
        P("row", None),
        P("col", "row"),
        P("row", None),
        P(None, "col"),
        P("col", None),
        P(None, "row"),
    )
    return jax.shard_map(
        local,
        mesh=mesh,
        in_specs=placed,
        out_specs=(P("row", None), P(None, "col"), P("col", None), P(None, "row")),
        check_vma=False,
    )
```

```python
import functools
import math

import jax
import jax.numpy as jnp
from jax import lax
from jax.experimental import pallas as pl
from jax.experimental.pallas import tpu as pltpu
from jax.sharding import PartitionSpec as P

HD = 128
HEADS = 64
KVH = 4

SCALE = 0.5
BF = jnp.bfloat16
F32 = jnp.float32


def mm(left, right, a, b):
    return lax.dot_general(
        left, right, (((a,), (b,)), ((), ())), preferred_element_type=F32
    )


def kernel(
    n_row,
    n_col,
    lengths_hbm,
    forget_hbm,
    x_hbm,
    cot_hbm,
    wq_hbm,
    wk_hbm,
    wv_hbm,
    wo_hbm,
    qd_hbm,
    up_hbm,
    od_hbm,
    ou_hbm,
    dq_ref,
    pieces_ref,
    du_ref,
    x,
    cot,
    wq,
    wkv,
    wo,
    qd,
    up,
    od,
    ou,
    red,
    chunk_send,
    chunk_recv,
    small_send,
    small_recv,
    fac_send,
    fac_recv,
    fac_all,
    piece_send,
    piece_recv,
    piece_all,
    lengths_ref,
    forget_ref,
    load_sem,
    wq_sem,
    wo_sem,
    chunk_ss,
    chunk_rs,
    small_ss,
    small_rs,
    fac_ss,
    fac_rs,
    all_ss,
    all_rs,
    piece_ss,
    piece_rs,
    gat_ss,
    gat_rs,
):
    me = lax.axis_index("row")
    mc = lax.axis_index("col")
    n_chunk, depth, width = wq.shape
    rank = qd.shape[0]
    tokens = x.shape[0]
    blk = tokens // n_row
    heads = n_chunk * width // HD
    per = width // HD
    inverse = 1.0 / math.sqrt(HD)
    group = lax.div(mc * heads, HEADS // KVH)
    group_cols = pl.ds(pl.multiple_of(group * HD, HD), HD)

    def row_peer(d):
        return lax.rem(me + d, n_row)

    def col_peer(d):
        return lax.rem(mc + d, n_col)

    def load_wq(c):
        return pltpu.make_async_copy(
            wq_hbm.at[:, pl.ds(c * width, width)], wq.at[c], wq_sem.at[c]
        )

    def load_wo(c):
        return pltpu.make_async_copy(
            wo_hbm.at[pl.ds(c * width, width), :], wo.at[c], wo_sem.at[c]
        )

    def up_load(c):
        return pltpu.make_async_copy(
            up_hbm.at[:, pl.ds(c * width, width)], up.at[c], load_sem.at[8 + c]
        )

    def od_load(c):
        return pltpu.make_async_copy(
            od_hbm.at[:, pl.ds(c * width, width)], od.at[c], load_sem.at[8 + n_chunk + c]
        )

    load_x = pltpu.make_async_copy(x_hbm, x, load_sem.at[0])
    load_qd = pltpu.make_async_copy(qd_hbm, qd, load_sem.at[1])
    load_k = pltpu.make_async_copy(wk_hbm.at[:, group_cols], wkv.at[0], load_sem.at[2])
    load_v = pltpu.make_async_copy(wv_hbm.at[:, group_cols], wkv.at[1], load_sem.at[3])
    load_cot = pltpu.make_async_copy(cot_hbm, cot, load_sem.at[4])
    load_ou = pltpu.make_async_copy(ou_hbm, ou, load_sem.at[5])
    load_len = pltpu.make_async_copy(lengths_hbm, lengths_ref, load_sem.at[6])
    load_forget = pltpu.make_async_copy(forget_hbm, forget_ref, load_sem.at[7])
    load_x.start()
    load_qd.start()
    for c in range(n_chunk):
        up_load(c).start()
    for c in range(n_chunk):
        load_wq(c).start()
    load_k.start()
    load_v.start()
    load_cot.start()
    load_ou.start()
    for c in range(n_chunk):
        od_load(c).start()
    load_len.start()
    load_forget.start()
    for c in range(n_chunk):
        load_wo(c).start()

    barrier = pltpu.get_barrier_semaphore()
    for d in range(1, n_row):
        pl.semaphore_signal(
            barrier, inc=1, device_id={"row": row_peer(d)}, device_id_type=pl.DeviceIdType.MESH
        )
    for d in range(1, n_col):
        pl.semaphore_signal(
            barrier, inc=1, device_id={"col": col_peer(d)}, device_id_type=pl.DeviceIdType.MESH
        )

    def remote(src, dst, send, recv, where):
        return pltpu.make_async_remote_copy(
            src_ref=src,
            dst_ref=dst,
            send_sem=send,
            recv_sem=recv,
            device_id=where,
            device_id_type=pl.DeviceIdType.MESH,
        )

    def chunk_copy(c, d):
        p = row_peer(d)
        return remote(
            chunk_send.at[c, p], chunk_recv.at[c, d], chunk_ss.at[c, d], chunk_rs.at[c, d], {"row": p}
        )

    def small_copy(d):
        p = row_peer(d)
        return remote(small_send.at[p], small_recv.at[d], small_ss.at[d], small_rs.at[d], {"row": p})

    def fac_copy(j, d):
        return remote(
            fac_send.at[j], fac_recv.at[j, d], fac_ss.at[j, d], fac_rs.at[j, d], {"col": col_peer(d)}
        )

    def all_copy(j, d, owner):
        return remote(
            fac_all.at[j, me], fac_all.at[j, owner], all_ss.at[j, d], all_rs.at[j, d], {"row": row_peer(d)}
        )

    def piece_copy(j, d):
        p = row_peer(d)
        return remote(
            piece_send.at[j, p], piece_recv.at[j, d], piece_ss.at[j, d], piece_rs.at[j, d], {"row": p}
        )

    def gat_copy(j, d, owner):
        return remote(
            piece_all.at[j, me], piece_all.at[j, owner], gat_ss.at[j, d], gat_rs.at[j, d], {"row": row_peer(d)}
        )

    quarter = blk // 4
    share = piece_send.shape[2]

    def send_factor(j, factor):
        packed = jnp.concatenate(
            [factor[i * quarter : (i + 1) * quarter] for i in range(4)], axis=1
        )
        fac_send[j] = packed.astype(BF)
        for d in range(1, n_col):
            fac_copy(j, d).start()

    def spread_factor(j):
        total = fac_send[j].astype(F32)
        for d in range(1, n_col):
            fac_copy(j, d).wait_recv()
            total = total + fac_recv[j, d].astype(F32)
        fac_all[j, me] = total.astype(BF)
        for d in range(1, n_row):
            all_copy(j, d, me).start()

    def factor_everywhere(j):
        for d in range(1, n_row):
            all_copy(j, d, row_peer(n_row - d)).wait_recv()
        blocks = []
        for r in range(n_row):
            block = fac_all[j, r].astype(F32)
            blocks.append(
                jnp.concatenate([block[:, i * rank : (i + 1) * rank] for i in range(4)], axis=0)
            )
        return blocks

    def send_piece(j, piece):
        for r in range(n_row):
            piece_send[j, r] = piece[r * share : (r + 1) * share].astype(BF)
        for d in range(1, n_row):
            piece_copy(j, d).start()

    def spread_piece(j):
        total = piece_send[j, me].astype(F32)
        for d in range(1, n_row):
            piece_copy(j, d).wait_recv()
            total = total + piece_recv[j, d].astype(F32)
        piece_all[j, me] = total.astype(BF)
        for d in range(1, n_row):
            gat_copy(j, d, me).start()

    def finish_piece(j):
        for d in range(1, n_row):
            gat_copy(j, d, row_peer(n_row - d)).wait_recv()
        for r in range(n_row):
            first = j * rank + r * share
            pieces_ref[first : first + share, :] = piece_all[j, r].astype(F32)

    load_x.wait()
    load_qd.wait()
    for c in range(n_chunk):
        up_load(c).wait()
    lowrank = mm(x[...], qd[...], 1, 1)
    red[0] = lowrank.astype(BF)
    pl.semaphore_wait(barrier, n_row + n_col - 2)

    @pl.loop(0, n_chunk)
    def _(c):
        pltpu.make_async_copy(
            wq_hbm.at[:, pl.ds(0, width)], wq.at[c], wq_sem.at[c]
        ).wait()
        term = mm(x[...], wq[c], 1, 0) + SCALE * mm(red[0], up[c], 1, 0)
        chunk_send[c] = term.astype(BF).reshape(n_row, blk, width)
        for d in range(1, n_row):
            chunk_copy(c, d).start()

    load_k.wait()
    load_v.wait()
    small_send[:, :, 0:HD] = mm(x[...], wkv[0], 1, 0).astype(BF).reshape(n_row, blk, HD)
    small_send[:, :, HD : 2 * HD] = mm(x[...], wkv[1], 1, 0).astype(BF).reshape(n_row, blk, HD)
    load_cot.wait()
    load_ou.wait()
    for c in range(n_chunk):
        od_load(c).wait()
    red[1] = mm(cot[...], ou[...], 1, 1).astype(BF)
    small_send[:, :, 2 * HD :] = jnp.concatenate(
        [red[0], red[1], jnp.zeros((tokens, HD - 2 * rank), BF)], axis=1
    ).reshape(n_row, blk, HD)
    for d in range(1, n_row):
        small_copy(d).start()

    @pl.loop(0, n_chunk)
    def _(c):
        pltpu.make_async_copy(
            wo_hbm.at[pl.ds(0, width), :], wo.at[c], wo_sem.at[c]
        ).wait()
        term = mm(cot[...], wo[c], 1, 1) + SCALE * mm(red[1], od[c], 1, 0)
        chunk_send[n_chunk + c] = term.astype(BF).reshape(n_row, blk, width)
        for d in range(1, n_row):
            chunk_copy(n_chunk + c, d).start()

    def chunk_sum(c):
        total = chunk_send[c, me].astype(F32)
        for d in range(1, n_row):
            chunk_copy(c, d).wait_recv()
            total = total + chunk_recv[c, d].astype(F32)
        return total

    def sign_of(first):
        lane = lax.broadcasted_iota(jnp.int32, (blk, tokens), 1)
        sub = lax.broadcasted_iota(jnp.int32, (blk, tokens), 0)
        picked = jnp.where(lane == sub + first, forget_ref[...], 0)
        return (1 - 2 * jnp.sum(picked, axis=1, keepdims=True)).astype(F32)

    load_len.wait()
    load_forget.wait()
    sign = sign_of(me * blk)

    stacked = []
    for c in range(n_chunk):
        part = chunk_sum(c).astype(BF)
        for h in range(per):
            stacked.append(part[:, h * HD : (h + 1) * HD])
    query = jnp.concatenate(stacked, axis=0)
    small = small_send[me].astype(F32)
    for d in range(1, n_row):
        small_copy(d).wait_recv()
        small = small + small_recv[d].astype(F32)
    key = small[:, 0:HD].astype(BF)
    value = small[:, HD : 2 * HD].astype(BF)
    in_low = small[:, 2 * HD : 2 * HD + rank].astype(BF)
    grad_low = (small[:, 2 * HD + rank : 2 * HD + 2 * rank] * sign).astype(BF)

    rows = heads * blk
    pos_q = lax.rem(lax.broadcasted_iota(jnp.int32, (rows, blk), 0), blk)
    pos_k = lax.broadcasted_iota(jnp.int32, (rows, blk), 1)
    seg_q = jnp.zeros((rows, blk), jnp.int32)
    seg_k = jnp.zeros((rows, blk), jnp.int32)
    end = 0
    for i in range(lengths_ref.shape[1]):
        end = end + lengths_ref[0, i]
        seg_q = seg_q + (pos_q >= end).astype(jnp.int32)
        seg_k = seg_k + (pos_k >= end).astype(jnp.int32)
    allowed = (seg_q == seg_k) & (pos_k <= pos_q)
    scores = mm(query, key, 1, 1) * inverse
    numer = jnp.where(allowed, jnp.exp(scores), 0.0)
    softmax = numer / jnp.sum(numer, axis=1, keepdims=True)
    hidden = mm(softmax.astype(BF), value, 1, 0).astype(BF)
    hidden_flat = jnp.concatenate([hidden[h * blk : (h + 1) * blk] for h in range(heads)], axis=1)
    hidden_factor = mm(hidden_flat[:, 0:width], od[0], 1, 1)
    for c in range(1, n_chunk):
        hidden_factor = hidden_factor + mm(hidden_flat[:, c * width : (c + 1) * width], od[c], 1, 1)
    send_factor(1, hidden_factor)
    send_piece(1, SCALE * mm(grad_low, hidden_flat, 0, 0))
    signs = [sign_of(r * blk) for r in range(n_row)]

    query_factor = jnp.zeros((blk, rank), F32)
    up_parts = []
    span = per * blk
    for c in range(n_chunk):
        part = (chunk_sum(n_chunk + c) * sign).astype(BF)
        hidden_grad = jnp.concatenate([part[:, h * HD : (h + 1) * HD] for h in range(per)], axis=0)
        soft = softmax[c * span : (c + 1) * span]
        prob_grad = mm(hidden_grad, value, 1, 1)
        score_grad = soft * (prob_grad - jnp.sum(prob_grad * soft, axis=1, keepdims=True))
        query_grad = (mm(score_grad.astype(BF), key, 1, 0) * inverse).astype(BF)
        flat = jnp.concatenate([query_grad[h * blk : (h + 1) * blk] for h in range(per)], axis=1)
        query_factor = query_factor + mm(flat, up[c], 1, 1)
        up_parts.append(SCALE * mm(in_low, flat, 0, 0))
    send_factor(0, query_factor)
    send_piece(0, jnp.concatenate(up_parts, axis=1))

    spread_factor(1)
    spread_factor(0)
    spread_piece(1)
    spread_piece(0)
    blocks = [(b * s).astype(BF) for b, s in zip(factor_everywhere(1), signs)]
    du_ref[...] = SCALE * mm(jnp.concatenate(blocks, axis=0), cot[...], 0, 0)
    blocks = [b.astype(BF) for b in factor_everywhere(0)]
    dq_ref[...] = SCALE * mm(jnp.concatenate(blocks, axis=0), x[...], 0, 0)
    finish_piece(1)
    finish_piece(0)

    for d in range(1, n_row):
        for c in range(2 * n_chunk):
            chunk_copy(c, d).wait_send()
        small_copy(d).wait_send()
        for j in range(2):
            all_copy(j, d, me).wait_send()
            piece_copy(j, d).wait_send()
            gat_copy(j, d, me).wait_send()
    for d in range(1, n_col):
        for j in range(2):
            fac_copy(j, d).wait_send()


def writer(dq, pieces, du, o_qd, o_up, o_od, o_ou, sem):
    rank = dq.shape[0]
    moves = [
        pltpu.make_async_copy(dq, o_qd, sem.at[0]),
        pltpu.make_async_copy(du, o_ou, sem.at[1]),
        pltpu.make_async_copy(pieces.at[pl.ds(0, rank)], o_up, sem.at[2]),
        pltpu.make_async_copy(pieces.at[pl.ds(rank, rank)], o_od, sem.at[3]),
    ]
    for move in moves:
        move.start()
    for move in moves:
        move.wait()


def local(
    activations,
    cotangent,
    forget,
    lengths,
    query_weight,
    key_weight,
    value_weight,
    output_projection_weight,
    query_down,
    query_up,
    output_down,
    output_up,
):
    n_row, n_col = lax.axis_size("row"), lax.axis_size("col")
    tokens, depth = activations.shape
    cols = query_weight.shape[1]
    rank = query_down.shape[1]
    blk = tokens // n_row
    width = min(256, cols)
    n_chunk = cols // width
    share = rank // n_row
    hbm = pl.BlockSpec(memory_space=pltpu.HBM)
    vmem = pl.BlockSpec(memory_space=pltpu.VMEM)
    dma = pltpu.SemaphoreType.DMA
    dq, pieces, du = pl.pallas_call(
        functools.partial(kernel, n_row, n_col),
        out_shape=(
            jax.ShapeDtypeStruct((rank, depth), F32),
            jax.ShapeDtypeStruct((2 * rank, cols), F32),
            jax.ShapeDtypeStruct((rank, depth), F32),
        ),
        in_specs=[hbm] * 12,
        out_specs=(vmem, vmem, vmem),
        scratch_shapes=[
            pltpu.VMEM((tokens, depth), BF),
            pltpu.VMEM((tokens, depth), BF),
            pltpu.VMEM((n_chunk, depth, width), BF),
            pltpu.VMEM((2, depth, HD), BF),
            pltpu.VMEM((n_chunk, width, depth), BF),
            pltpu.VMEM((rank, depth), BF),
            pltpu.VMEM((n_chunk, rank, width), BF),
            pltpu.VMEM((n_chunk, rank, width), BF),
            pltpu.VMEM((rank, depth), BF),
            pltpu.VMEM((2, tokens, rank), BF),
            pltpu.VMEM((2 * n_chunk, n_row, blk, width), BF),
            pltpu.VMEM((2 * n_chunk, n_row, blk, width), BF),
            pltpu.VMEM((n_row, blk, 3 * HD), BF),
            pltpu.VMEM((n_row, blk, 3 * HD), BF),
            pltpu.VMEM((2, blk // 4, 4 * rank), BF),
            pltpu.VMEM((2, n_col, blk // 4, 4 * rank), BF),
            pltpu.VMEM((2, n_row, blk // 4, 4 * rank), BF),
            pltpu.VMEM((2, n_row, share, cols), BF),
            pltpu.VMEM((2, n_row, share, cols), BF),
            pltpu.VMEM((2, n_row, share, cols), BF),
            pltpu.SMEM(lengths.shape, jnp.int32),
            pltpu.VMEM((1, tokens), jnp.int32),
            dma((8 + 2 * n_chunk,)),
            dma((n_chunk,)),
            dma((n_chunk,)),
            dma((2 * n_chunk, n_row)),
            dma((2 * n_chunk, n_row)),
            dma((n_row,)),
            dma((n_row,)),
            dma((2, n_col)),
            dma((2, n_col)),
            dma((2, n_row)),
            dma((2, n_row)),
            dma((2, n_row)),
            dma((2, n_row)),
            dma((2, n_row)),
            dma((2, n_row)),
        ],
        compiler_params=pltpu.CompilerParams(
            collective_id=0, has_side_effects=True, vmem_limit_bytes=50 << 20
        ),
        name="unlearn_step",
    )(
        *(
            pltpu.with_memory_space_constraint(operand, pltpu.HBM)
            for operand in (
                lengths,
                forget.reshape(1, tokens),
                activations,
                cotangent,
                query_weight,
                key_weight,
                value_weight,
                output_projection_weight,
                query_down.T,
                query_up,
                output_down.T,
                output_up,
            )
        )
    )
    down_grad, up_grad, out_down_grad, out_up_grad = pl.pallas_call(
        writer,
        out_shape=(
            jax.ShapeDtypeStruct((rank, depth), F32),
            jax.ShapeDtypeStruct((rank, cols), F32),
            jax.ShapeDtypeStruct((rank, cols), F32),
            jax.ShapeDtypeStruct((rank, depth), F32),
        ),
        in_specs=[pl.BlockSpec(memory_space=pl.ANY)] * 3,
        out_specs=(hbm,) * 4,
        scratch_shapes=[dma((4,))],
        compiler_params=pltpu.CompilerParams(vmem_limit_bytes=1 << 20),
        name="write_outputs",
    )(dq, pieces, du)
    return down_grad.T, up_grad, out_down_grad.T, out_up_grad


def solution(mesh):
    placed = (
        P(None, "row"),
        P(None, "row"),
        P(),
        P("row", None),
        P("row", "col"),
        P("row", None),
        P("row", None),
        P("col", "row"),
        P("row", None),
        P(None, "col"),
        P("col", None),
        P(None, "row"),
    )
    return jax.shard_map(
        local,
        mesh=mesh,
        in_specs=placed,
        out_specs=(P("row", None), P(None, "col"), P("col", None), P(None, "row")),
        check_vma=False,
    )
```
